128 devices in a mesh: gx: 32 (over y, z_lo, x), yz: 4 (over z_hi, core).
Axes of the slice: x: 4, y: 4, z: 4 (z_hi: 2, z_lo: 2; z = z_hi * 2 + z_lo), core: 2. Of those that a mesh axis runs over, the one named last changes fastest.
Arguments:
- design: float32 [128, 64, 128], P('gx', 'yz'), may hold values from 0.2 to 1
- passive: int32 [128, 64, 128], P('gx', 'yz'), may hold values 0 or 1
- support: int32 [128, 64, 128], P('gx', 'yz'), may hold values 0 or 1
- warm_modes: float32 [3, 12, 128, 64, 128], P(None, None, 'gx', 'yz'), may hold values from -6 to 6
Outputs:
- mode_shapes: float32 [3, 12, 128, 64, 128], P(None, None, 'gx', 'yz')
- projected: float32 [12, 12], replicated
The draws below stay inside these ranges and needn't reach their ends.
All inputs are finite; a program needn't handle non-finite values. No bound on the sum of `passive` or of `support` on one device may be relied on, other than what follows from the above.
Results may differ from the reference program's by a relative error of at most 0.0001.
Values sent between devices are 32-bit elements; how exact they have to be, the bound alone decides.
No kernel may reach another device: no remote copies, remote signals or barrier semaphores. Data moves between devices by JAX's collectives and lax.ppermute only.
A program may use at most 128 MiB of HBM per device.

```python
import jax
import jax.numpy as jnp
import numpy as np
from jax import lax

MODES = 12
SWEEPS = 4
DEGREE = 2
NX = 128
NY = 64
NZ = 128


def place_ends(entries, key, least, top_value):
    dims = entries.shape
    place = [jax.random.randint(jax.random.fold_in(key, axis), (), 0, dims[axis]) for axis in range(len(dims))]
    entries = entries.at[tuple(place)].set(least)
    longest = dims.index(max(dims))
    place[longest] = (place[longest] + 1) % dims[longest]
    return entries.at[tuple(place)].set(top_value)


def shard_levels(key, shape, pieces, least, top_value):
    def one(axis_at, shards_of):
        heights = jax.random.uniform(jax.random.fold_in(jax.random.fold_in(key, 6), axis_at), (shards_of,), jnp.float32, least / len(pieces), top_value / len(pieces))
        return jnp.repeat(jnp.exp(heights), shape[axis_at] // shards_of).reshape((-1,) + (1,) * (len(shape) - axis_at - 1))

    level = one(*pieces[0])
    for cut in pieces[1:]:
        level = level * one(*cut)
    return level


def normal_values(key, shape, scale, most, shards=(), kind=jnp.bfloat16):
    result = scale * jax.random.normal(key, shape, jnp.float32)
    if shards:
        result = result * shard_levels(key, shape, shards, -0.22, 0.18)
    return jnp.clip(result, -most, most).astype(kind)


def setup_inputs(seed: int = 0) -> dict:
    splits = jax.random.split(jax.random.key(seed), 5)
    return {
        "design": jnp.clip(0.2 + 0.8 * jax.random.uniform(splits[0], (NX, NY, NZ), jnp.float32) ** shard_levels(splits[0], (NX, NY, NZ), ((0, 32), (1, 4)), -0.2, 0.2), 0.2, 1.0),
        "passive": place_ends((jax.random.randint(splits[1], (NX, NY, NZ), 0, 10) < 1).astype(jnp.int32), jax.random.fold_in(splits[1], 1), 0, 1),
        "support": place_ends((jax.random.randint(splits[2], (NX, NY, NZ), 0, 16) < 1).astype(jnp.int32), jax.random.fold_in(splits[2], 1), 0, 1),
        "warm_modes": normal_values(splits[3], (3, MODES, NX, NY, NZ), 1.0, 6.0, ((2, 32), (3, 4)), jnp.float32),
    }


soft_modulus = 0.001
filter_weight = 2.0
cut_ratio = 0.02
highest_precision = lax.Precision.HIGHEST

def element_matrix():
    poisson = 0.3
    lame_first = poisson / ((1.0 + poisson) * (1.0 - 2.0 * poisson))
    lame_shear = 0.5 / (1.0 + poisson)
    elastic = np.zeros((6, 6))
    elastic[:3, :3] = lame_first
    for direction in range(3):
        elastic[direction, direction] += 2.0 * lame_shear
        elastic[direction + 3, direction + 3] = lame_shear
    corner_signs = np.array([[a_side, b_side, c_side] for a_side in (0, 1) for b_side in (0, 1) for c_side in (0, 1)]) * 2.0 - 1.0
    gauss_points = np.array([-1.0, 1.0]) / np.sqrt(3.0)
    stiffness = np.zeros((24, 24))
    for first_point in gauss_points:
        for second_point in gauss_points:
            for third_point in gauss_points:
                natural = np.array([first_point, second_point, third_point])
                gradients = np.zeros((8, 3))
                for corner in range(8):
                    for direction in range(3):
                        product = corner_signs[corner, direction] / 8.0
                        for other in range(3):
                            if other != direction:
                                product = product * (1.0 + corner_signs[corner, other] * natural[other])
                        gradients[corner, direction] = 2.0 * product
                strain = np.zeros((6, 24))
                for corner in range(8):
                    strain[0, corner] = gradients[corner, 0]
                    strain[1, 8 + corner] = gradients[corner, 1]
                    strain[2, 16 + corner] = gradients[corner, 2]
                    strain[3, corner] = gradients[corner, 1]
                    strain[3, 8 + corner] = gradients[corner, 0]
                    strain[4, 8 + corner] = gradients[corner, 2]
                    strain[4, 16 + corner] = gradients[corner, 1]
                    strain[5, corner] = gradients[corner, 2]
                    strain[5, 16 + corner] = gradients[corner, 0]
                stiffness = stiffness + strain.T @ elastic @ strain * 0.125
    return stiffness

def upper_value():
    return 8.0 * float(np.max(np.sum(np.abs(element_matrix()), axis=1)))

def jacobi(extended, design, neighbours, inside):
    padded = jnp.pad(extended, ((0, 0), (0, 0), (1, 1)))
    beside_all = padded[2:, 1:-1, 1:-1] + padded[:-2, 1:-1, 1:-1]
    beside_all = beside_all + padded[1:-1, 2:, 1:-1] + padded[1:-1, :-2, 1:-1]
    beside_all = beside_all + padded[1:-1, 1:-1, 2:] + padded[1:-1, 1:-1, :-2]
    return inside * (design + filter_weight * beside_all) / (1.0 + filter_weight * neighbours)

def neighbour_count(x_global, y_global, depth, x_total, y_total):
    z_global = jnp.arange(depth)
    x_part = (x_global > 0).astype(jnp.float32) + (x_global < x_total - 1).astype(jnp.float32)
    y_part = (y_global > 0).astype(jnp.float32) + (y_global < y_total - 1).astype(jnp.float32)
    z_part = (z_global > 0).astype(jnp.float32) + (z_global < depth - 1).astype(jnp.float32)
    return x_part[:, None, None] + y_part[None, :, None] + z_part[None, None, :]

def nodal_mass(density_ext, x_cells, y_cells, z_cells):
    lumped = jnp.zeros((x_cells, y_cells, z_cells), jnp.float32)
    for x_side in (0, 1):
        for y_side in (0, 1):
            for z_side in (0, 1):
                lumped = lumped + density_ext[1 - x_side:1 - x_side + x_cells, 1 - y_side:1 - y_side + y_cells, 1 - z_side:1 - z_side + z_cells]
    return lumped / 8.0

def node_forces(node_block, moduli):
    stiffness = jnp.asarray(element_matrix(), jnp.float32)
    planes = moduli.shape[0]
    y_cells = moduli.shape[1]
    z_cells = moduli.shape[2]
    columns = node_block.shape[1]

    def add_plane(plane_index, accumulated):
        slab_plane = lax.dynamic_slice_in_dim(node_block, plane_index, 2, axis=2)
        corner_list = []
        for x_side in (0, 1):
            for y_side in (0, 1):
                for z_side in (0, 1):
                    corner_list.append(slab_plane[:, :, x_side, y_side:y_side + y_cells, z_side:z_side + z_cells])
        gathered = jnp.stack(corner_list, axis=1).reshape(24, columns, y_cells, z_cells)
        plane_moduli = lax.dynamic_index_in_dim(moduli, plane_index, 0, keepdims=False)
        element_force = jnp.einsum('ab,bmyz->amyz', stiffness, gathered, precision=highest_precision) * plane_moduli
        element_force = element_force.reshape(3, 8, columns, y_cells, z_cells)
        for x_side in (0, 1):
            spread = jnp.zeros((3, columns, y_cells + 1, z_cells + 1), jnp.float32)
            for y_side in (0, 1):
                for z_side in (0, 1):
                    corner = 4 * x_side + 2 * y_side + z_side
                    spread = spread + jnp.pad(element_force[:, corner], ((0, 0), (0, 0), (y_side, 1 - y_side), (z_side, 1 - z_side)))
            current = lax.dynamic_slice_in_dim(accumulated, plane_index + x_side, 1, axis=2)
            accumulated = lax.dynamic_update_slice_in_dim(accumulated, current + spread[:, :, None], plane_index + x_side, axis=2)
        return accumulated
    return lax.fori_loop(0, planes, add_plane, jnp.zeros(node_block.shape, jnp.float32))

def apply_operator(vectors, scaling, moduli_ext):
    node_block = jnp.pad(scaling * vectors, ((0, 0), (0, 0), (1, 1), (1, 1), (1, 1)))
    forces = node_forces(node_block, moduli_ext)
    return scaling * forces[:, :, 1:-1, 1:-1, 1:-1]

def reference(design, passive, support, warm_modes):
    x_cells, y_cells, z_cells = design.shape
    neighbours = neighbour_count(jnp.arange(x_cells), jnp.arange(y_cells), z_cells, x_cells, y_cells)
    filtered = design
    for sweep_index in range(SWEEPS):
        extended = jnp.pad(filtered, ((1, 1), (1, 1), (0, 0)))
        filtered = jacobi(extended, design, neighbours, 1.0)
    density = jnp.where(passive == 1, jnp.float32(1.0), filtered)
    moduli = soft_modulus + (1.0 - soft_modulus) * density ** 3
    density_ext = jnp.pad(density, ((1, 0), (1, 0), (1, 0)))
    moduli_ext = jnp.pad(moduli, ((1, 0), (1, 0), (1, 0)))
    lumped = nodal_mass(density_ext, x_cells, y_cells, z_cells)
    scaling = (1.0 - support.astype(jnp.float32)) / jnp.sqrt(lumped)
    upper_edge = upper_value()
    lower_edge = cut_ratio * upper_edge
    center_value = 0.5 * (upper_edge + lower_edge)
    half_width = 0.5 * (upper_edge - lower_edge)
    previous = warm_modes * (1.0 - support.astype(jnp.float32))
    latest = (apply_operator(previous, scaling, moduli_ext) - center_value * previous) / half_width
    for degree_index in range(DEGREE - 1):
        following = 2.0 * (apply_operator(latest, scaling, moduli_ext) - center_value * latest) / half_width - previous
        previous = latest
        latest = following
    image = apply_operator(latest, scaling, moduli_ext)
    total_dof = 3.0 * x_cells * y_cells * z_cells
    gram = jnp.einsum('cixyz,cjxyz->ij', latest, latest, precision=highest_precision) / total_dof
    stiff = jnp.einsum('cixyz,cjxyz->ij', latest, image, precision=highest_precision) / total_dof
    lower = jnp.linalg.cholesky(gram)
    inverse = jax.scipy.linalg.solve_triangular(lower, jnp.eye(gram.shape[0], dtype=jnp.float32), lower=True)
    ortho = jnp.einsum('ji,cixyz->cjxyz', inverse, latest, precision=highest_precision)
    projected = jnp.dot(jnp.dot(inverse, stiff, precision=highest_precision), inverse.T, precision=highest_precision)
    return (scaling * ortho, projected)
```

```python
import jax
import jax.numpy as jnp
import numpy as np
from jax import lax
from jax.experimental import pallas as pl
from jax.experimental.pallas import tpu as pltpu
from jax.sharding import Mesh
from jax.sharding import PartitionSpec as P

MODES = 12
LOW, HIGH = 2, 3
Y, ZL, X, ZH, C = "gx_0", "gx_1", "gx_2", "yz_0", "yz_1"
GX = (Y, ZL, X)
YZ = (ZH, C)
ROWS = 24

POISSON = 0.3
LAME = POISSON / ((1.0 + POISSON) * (1.0 - 2.0 * POISSON))
SHEAR = 0.5 / (1.0 + POISSON)
SOFT = 0.001


def element_matrix():
    elastic = np.zeros((6, 6))
    elastic[:3, :3] = LAME
    for d in range(3):
        elastic[d, d] += 2.0 * SHEAR
        elastic[d + 3, d + 3] = SHEAR
    signs = np.array([[a, b, c] for a in (0, 1) for b in (0, 1) for c in (0, 1)]) * 2.0 - 1.0
    points = np.array([-1.0, 1.0]) / np.sqrt(3.0)
    stiffness = np.zeros((24, 24))
    for p in points:
        for q in points:
            for r in points:
                natural = np.array([p, q, r])
                grad = np.zeros((8, 3))
                for k in range(8):
                    for d in range(3):
                        v = signs[k, d] / 8.0
                        for o in range(3):
                            if o != d:
                                v = v * (1.0 + signs[k, o] * natural[o])
                        grad[k, d] = 2.0 * v
                strain = np.zeros((6, 24))
                for k in range(8):
                    for d in range(3):
                        strain[d, 8 * d + k] = grad[k, d]
                    strain[3, k], strain[3, 8 + k] = grad[k, 1], grad[k, 0]
                    strain[4, 8 + k], strain[4, 16 + k] = grad[k, 2], grad[k, 1]
                    strain[5, k], strain[5, 16 + k] = grad[k, 2], grad[k, 0]
                stiffness = stiffness + strain.T @ elastic @ strain * 0.125
    return stiffness


UPPER = 8.0 * float(np.max(np.sum(np.abs(element_matrix()), axis=1)))
CENTER = 0.5 * (UPPER + 0.02 * UPPER)
HALF = 0.5 * (UPPER - 0.02 * UPPER)

KAPPA2 = 1.0 / 12.0
COEFS = (
    LAME / 16.0,
    2.0 * SHEAR / 16.0,
    SHEAR / 16.0,
    KAPPA2 * (LAME + 3.0 * SHEAR) / 4.0,
    KAPPA2 * LAME / 4.0,
    KAPPA2 * SHEAR / 4.0,
    KAPPA2 * KAPPA2 * (LAME + 4.0 * SHEAR),
)


def lanes(shape):
    return lax.broadcasted_iota(jnp.int32, shape, len(shape) - 1)


def sublanes(shape):
    return lax.broadcasted_iota(jnp.int32, shape, len(shape) - 2)


def filter_kernel(x_total, y_total, pos_ref, aux_ref, low_ref, high_ref, scale_ref, free_ref, coef_ref):
    x0, y0 = pos_ref[0], pos_ref[1]
    shape = (32, 128)
    lane, row = lanes(shape), sublanes(shape)
    first, last = lane == 0, lane == 127
    y_at = row + (y0 - 8)
    y_in = (y_at >= 0) & (y_at < y_total)

    def load(k):
        return jnp.concatenate([low_ref[k], aux_ref[k], high_ref[k]], axis=0)

    def after_z(v):
        return jnp.where(last, 0.0, pltpu.roll(v, 127, axis=1))

    def before_z(v):
        return jnp.where(first, 0.0, pltpu.roll(v, 1, axis=1))

    part = jnp.where(first | last, 1.0, 2.0)
    part = part + jnp.where((y_at == 0) | (y_at == y_total - 1), 1.0, 2.0)
    inner = jnp.where(y_in, 1.0 / (1.0 + 2.0 * (part + 2.0)), 0.0)
    outer = jnp.where(y_in, 1.0 / (1.0 + 2.0 * (part + 1.0)), 0.0)
    y_on = jnp.where(y_in, 1.0, 0.0)

    def at_plane(k):
        x_at = x0 - 7 + k
        inside = (x_at >= 0) & (x_at < x_total)
        return inside, (x_at == 0) | (x_at == x_total - 1)

    inverse = []
    for k in range(18):
        inside, edge = at_plane(k)
        chosen = jnp.where(edge, outer, inner)
        inverse.append(jnp.where(inside, chosen, 0.0))
    design = [load(k) for k in range(18)]
    current = {k: design[k] for k in range(18)}
    for sweep in range(1, 5):
        step = {}
        for k in range(sweep, 18 - sweep):
            v = current[k]
            beside = current[k - 1] + current[k + 1]
            beside = beside + pltpu.roll(v, 31, axis=0) + pltpu.roll(v, 1, axis=0)
            beside = beside + after_z(v) + before_z(v)
            step[k] = (design[k] + 2.0 * beside) * inverse[k]
        current = step
    density = {}
    for k in range(4, 14):
        density[k] = jnp.where(load(18 + k - 4) > 0.5, 1.0, current[k])
    pos8 = sublanes((8, 128))

    def put(ref, index, v):
        ref[index + (slice(0, 16),)] = v[8:24]
        ref[index + (slice(16, 24),)] = jnp.where(pos8 < 4, v[24:32], v[0:8])

    for e in range(8):
        k = 5 + e
        inside, _ = at_plane(k)
        modulus = (SOFT + (1.0 - SOFT) * (density[k] * density[k] * density[k])) * y_on
        modulus = jnp.where(inside, modulus, 0.0)
        for c, factor in enumerate(COEFS):
            put(coef_ref, (c, e), modulus * factor)
    sums = {}
    for k in range(4, 14):
        v = density[k]
        v = v + before_z(v)
        sums[k] = v + pltpu.roll(v, 1, axis=0)
    for n in range(9):
        k = 5 + n
        inside, _ = at_plane(k)
        free = jnp.where(inside, (1.0 - load(28 + n)) * y_on, 0.0)
        lumped = (sums[k] + sums[k - 1]) * 0.125
        lumped = jnp.where(lumped > 0.0, lumped, 1.0)
        put(free_ref, (n,), free)
        put(scale_ref, (n,), free / jnp.sqrt(lumped))


def main_kernel(own_ref, xlow_ref, xhigh_ref, ylow_ref, yhigh_ref, scale_ref, free_ref, coef_ref,
                y2_ref, part_ref, v2_ref, f3_ref, y0_ref, y1_ref, flat_ref):
    shape = (ROWS, 128)
    lane = lanes(shape)
    first, last = lane == 0, lane == 127
    zero_tile = jnp.zeros((8, 128), jnp.float32)
    zero2 = jnp.zeros((2, 128), jnp.float32)

    def transforms(comps):
        out = []
        for u in comps:
            uz = jnp.where(last, 0.0, pltpu.roll(u, 127, axis=1))
            here = []
            for w in (u + uz, uz - u):
                wy = pltpu.roll(w, ROWS - 1, axis=0)
                here.append((w + wy, wy - w))
            out.append(((here[0][0], here[1][0]), (here[0][1], here[1][1])))
        return out

    def element(low, high, e, rows):
        def mode(c, x, y, z):
            a, b = low[c][y][z][:rows], high[c][y][z][:rows]
            return b - a if x else a + b

        k = [coef_ref[i, e, :rows] for i in range(7)]
        g = [[[[None, None], [None, None]], [[None, None], [None, None]]] for _ in range(3)]
        ux, vy, wz = mode(0, 1, 0, 0), mode(1, 0, 1, 0), mode(2, 0, 0, 1)
        trace = (ux + vy + wz) * k[0]
        g[0][1][0][0] = ux * k[1] + trace
        g[1][0][1][0] = vy * k[1] + trace
        g[2][0][0][1] = wz * k[1] + trace
        t = (mode(0, 0, 1, 0) + mode(1, 1, 0, 0)) * k[2]
        g[0][0][1][0] = t
        g[1][1][0][0] = t
        t = (mode(0, 0, 0, 1) + mode(2, 1, 0, 0)) * k[2]
        g[0][0][0][1] = t
        g[2][1][0][0] = t
        t = (mode(1, 0, 0, 1) + mode(2, 0, 1, 0)) * k[2]
        g[1][0][0][1] = t
        g[2][0][1][0] = t
        for (c, x, y, z), (d, p, q, r) in (
            ((0, 1, 1, 0), (2, 0, 1, 1)),
            ((1, 1, 1, 0), (2, 1, 0, 1)),
            ((0, 1, 0, 1), (1, 0, 1, 1)),
        ):
            a, b = mode(c, x, y, z), mode(d, p, q, r)
            g[c][x][y][z] = a * k[3] + b * k[4]
            g[d][p][q][r] = b * k[3] + a * k[4]
        a, b, c = mode(2, 1, 1, 0), mode(1, 1, 0, 1), mode(0, 0, 1, 1)
        total = a + b + c
        g[2][1][1][0] = (a + total) * k[5]
        g[1][1][0][1] = (b + total) * k[5]
        g[0][0][1][1] = (c + total) * k[5]
        for c in range(3):
            g[c][1][1][1] = mode(c, 1, 1, 1) * k[6]
        return g

    def to_low(g):
        out = []
        for c in range(3):
            out.append([[-g[c][1][y][z] if (y, z) == (0, 0) else g[c][0][y][z] - g[c][1][y][z]
                         for z in (0, 1)] for y in (0, 1)])
        return out

    def to_high(g):
        out = []
        for c in range(3):
            out.append([[g[c][1][y][z] if (y, z) == (0, 0) else g[c][0][y][z] + g[c][1][y][z]
                         for z in (0, 1)] for y in (0, 1)])
        return out

    def gather(a, b):
        out = []
        for c in range(3):
            if a is None:
                h = b[c]
            elif b is None:
                h = a[c]
            else:
                h = [[a[c][y][z] + b[c][y][z] for z in (0, 1)] for y in (0, 1)]
            along = []
            for z in (0, 1):
                s, d = h[0][z], h[1][z]
                near, far = s - d, s + d
                if near.shape[0] != ROWS:
                    near = jnp.concatenate([near, zero_tile], axis=0)
                    far = jnp.concatenate([far, zero_tile], axis=0)
                along.append(near + pltpu.roll(far, 1, axis=0))
            far = pltpu.roll(along[0] + along[1], 1, axis=1)
            out.append((along[0] - along[1]) + jnp.where(first, 0.0, far))
        return out

    def sweep(vector, start, stop, rows, ends, done):
        low = transforms(vector(start - 1 if ends else start))
        below = None
        p = start if ends else start + 1
        if not ends:
            high = transforms(vector(start + 1))
        while True:
            high = transforms(vector(p))
            g = element(low, high, p - 1 + LOW, rows)
            if p - 1 >= start:
                done(p - 1, gather(to_low(g), below))
            below = to_high(g)
            low = high
            p += 1
            if p > (stop + 1 if ends else stop):
                break
        if not ends:
            done(stop, gather(None, below))

    def per_mode(m, carry):
        for p in range(-LOW, 4 + HIGH):
            n = p + LOW
            for c in range(3):
                if p < 0:
                    rows = xlow_ref[c, m, p + LOW]
                elif p < 4:
                    rows = own_ref[c, m, p]
                else:
                    rows = xhigh_ref[c, m, p - 4]
                tile = jnp.concatenate([yhigh_ref[c, m, n], zero2, ylow_ref[c, m, n]], axis=0)
                y0_ref[c, n] = jnp.concatenate([rows, tile], axis=0)

        def v0(p):
            s = scale_ref[p + LOW]
            return [y0_ref[c, p + LOW] * s for c in range(3)]

        def y0(p, c):
            return y0_ref[c, p + LOW] * free_ref[p + LOW]

        def done1(p, f):
            s = scale_ref[p + LOW] * (1.0 / HALF)
            for c in range(3):
                y1_ref[c, p + 1] = f[c] * s - y0(p, c) * (CENTER / HALF)

        sweep(v0, -1, 5, ROWS, True, done1)

        def v1(p):
            s = scale_ref[p + LOW]
            return [y1_ref[c, p + 1] * s for c in range(3)]

        def done2(p, f):
            scale = scale_ref[p + LOW]
            s = scale * (2.0 / HALF)
            for c in range(3):
                y2 = f[c] * s - y1_ref[c, p + 1] * (2.0 * CENTER / HALF) - y0(p, c)
                if p < 4:
                    y2_ref[c, m, p] = y2[:16]
                v2_ref[m, 5 * c + p] = y2 * scale

        sweep(v1, 0, 4, ROWS, True, done2)

        def v2(p):
            return [v2_ref[m, 5 * c + p] for c in range(3)]

        def done3(p, f):
            for c in range(3):
                f3_ref[m, 5 * c + p] = f[c]

        sweep(v2, 0, 4, 16, False, done3)
        return carry

    lax.fori_loop(0, MODES, per_mode, 0)

    flat_ref[...] = jnp.zeros_like(flat_ref)

    def products(base, left, right, count):
        for ii, jj in ((0, 0), (6, 6), (0, 6)):
            pairs = [(i, j) for i in range(ii, ii + 6) for j in range(jj, jj + 6) if i <= j]

            def body(q, acc):
                a = {i: left(q, i) for i in range(ii, ii + 6)}
                b = {j: right(q, j) for j in range(jj, jj + 6)}
                return tuple(s + a[i] * b[j] for s, (i, j) in zip(acc, pairs))

            acc = lax.fori_loop(0, count, body, tuple(zero_tile for _ in pairs))
            for s, (i, j) in zip(acc, pairs):
                r = jnp.sum(s, axis=0, keepdims=True)
                flat_ref[pl.ds(base + 16 * i + j, 1), :] = r
                if i != j:
                    flat_ref[pl.ds(base + 16 * j + i, 1), :] = r

    def own(q, i):
        return y2_ref[q // 8, i, (q // 2) % 4, pl.ds(pl.multiple_of((q % 2) * 8, 8), 8)]

    products(0, own, own, 24)

    def tile_of(ref):
        return lambda q, i: ref[i, q // 3, pl.ds(pl.multiple_of((q % 3) * 8, 8), 8)]

    products(192, tile_of(v2_ref), tile_of(f3_ref), 45)
    sums = jnp.sum(flat_ref[...], axis=1, keepdims=True)
    lane16 = lanes((16, 128))
    result = jnp.zeros((16, 128), jnp.float32)
    for k in range(2):
        for i in range(MODES):
            column = sums[192 * k + 16 * i : 192 * k + 16 * i + 16]
            result = jnp.where(lane16 == 16 * k + i, column, result)
    part_ref[...] = result


def tail_kernel(total_dof, sum_ref, y2_ref, scale_ref, out_ref, projected_ref, w_ref):
    shape = (16, 128)
    lane, row = lanes(shape), sublanes(shape)
    total = sum_ref[...] * (1.0 / total_dof)
    stiff = total[:, 16:32]
    work = jnp.where(lane < 16, total, jnp.where(lane - 16 == row, 1.0, 0.0))
    for k in range(MODES):
        pivot = work[k : k + 1, k : k + 1]
        scaled = work * (1.0 / jnp.sqrt(pivot))
        line = scaled[k : k + 1, :]
        column = jnp.where(row > k, jnp.broadcast_to(scaled[:, k : k + 1], shape), 0.0)
        work = jnp.where(row == k, scaled, work - column * line)
    inverse = work[:, 16:32]
    inverse = jnp.where(sublanes((16, 16)) < MODES, inverse, 0.0)
    half = jnp.dot(inverse, stiff, precision=lax.Precision.HIGHEST)
    full = lax.dot_general(half, inverse, (((1,), (1,)), ((), ())), precision=lax.Precision.HIGHEST)
    projected_ref[...] = full[:MODES, :MODES]
    for j in range(MODES):
        for i in range(j + 1):
            w_ref[MODES * j + i] = jnp.broadcast_to(work[j : j + 1, 16 + i : 17 + i], (8, 128))

    def body(q, carry):
        c, p, r = q // 8, (q // 2) % 4, pl.multiple_of((q % 2) * 8, 8)
        scale = scale_ref[p + LOW, pl.ds(r, 8)]
        y = [y2_ref[c, i, p, pl.ds(r, 8)] * scale for i in range(MODES)]
        for j in range(MODES):
            v = y[0] * w_ref[MODES * j]
            for i in range(1, j + 1):
                v = v + y[i] * w_ref[MODES * j + i]
            out_ref[c, j, p, pl.ds(r, 8)] = v
        return carry

    lax.fori_loop(0, 24, body, 0)


VMEM = pl.BlockSpec(memory_space=pltpu.VMEM)


def call(kernel, ins, outs, scratch=(), scalars=0):
    return pl.pallas_call(
        kernel,
        out_shape=tuple(jax.ShapeDtypeStruct(s, jnp.float32) for s in outs),
        in_specs=[pl.BlockSpec(memory_space=pltpu.SMEM)] * scalars + [VMEM] * (len(ins) - scalars),
        out_specs=tuple(VMEM for _ in outs),
        scratch_shapes=[pltpu.VMEM(s, jnp.float32) for s in scratch],
        compiler_params=pltpu.CompilerParams(vmem_limit_bytes=48 * 1024 * 1024),
    )(*ins)


def shift(value, axis, steps):
    count = lax.axis_size(axis)
    pairs = [(i, i + steps) for i in range(count) if 0 <= i + steps < count]
    return lax.ppermute(value, axis, pairs)


def all_sum(value):
    for axis, flip in (((C,), 1), ((X,), 1), ((X,), 3), ((Y,), 1), ((Y,), 3)):
        count = lax.axis_size(axis)
        value = value + lax.ppermute(value, axis, [(i, i ^ flip) for i in range(count)])
    for flip in (1, 3):
        pairs = []
        for zl in range(2):
            for zh in range(2):
                other = (2 * zh + zl) ^ flip
                pairs.append((2 * zl + zh, 2 * (other % 2) + other // 2))
        value = value + lax.ppermute(value, (ZL, ZH), pairs)
    return value


def on_device(design, passive, support, warm):
    x_cells, y_cells, z_cells = design.shape
    x_total = x_cells * lax.axis_size(GX)
    y_total = y_cells * lax.axis_size(YZ)
    position = jnp.stack([lax.axis_index(GX) * x_cells, lax.axis_index(YZ) * y_cells]).astype(jnp.int32)
    aux = jnp.stack([design, passive.astype(jnp.float32), support.astype(jnp.float32)])
    below = shift(aux, GX, 1)
    above = shift(aux, GX, -1)
    below2 = shift(design[1:4], GX, 2)
    above2 = shift(design[0:3], GX, -2)
    wide = jnp.concatenate(
        [below2, below[0], design, above[0], above2,
         below[1, 1:], aux[1], above[1, :3],
         below[2, 2:], aux[2], above[2, :3]], axis=0)
    wide_low = shift(wide[:, 8:], YZ, 1)
    wide_high = shift(wide[:, :8], YZ, -1)
    xlow = shift(warm[:, :, 2:], GX, 1)
    xhigh = shift(warm[:, :, :3], GX, -1)
    rows_up = jnp.concatenate([xlow[:, :, :, 14:], warm[:, :, :, 14:], xhigh[:, :, :, 14:]], axis=2)
    rows_down = jnp.concatenate([xlow[:, :, :, :4], warm[:, :, :, :4], xhigh[:, :, :, :4]], axis=2)
    ylow = shift(rows_up, YZ, 1)
    yhigh = shift(rows_down, YZ, -1)

    def filtering(*refs):
        filter_kernel(x_total, y_total, *refs)

    scale, free, coef = call(
        filtering, (position, wide, wide_low, wide_high),
        ((9, ROWS, 128), (9, ROWS, 128), (7, 8, ROWS, 128)), scalars=1)
    y2, part = call(
        main_kernel, (warm, xlow, xhigh, ylow, yhigh, scale, free, coef),
        (warm.shape, (16, 128)),
        ((MODES, 15, ROWS, 128), (MODES, 15, ROWS, 128), (3, 9, ROWS, 128), (3, 7, ROWS, 128), (384, 128)))
    total = all_sum(part)

    def finish(*refs):
        tail_kernel(3.0 * x_total * y_total * z_cells, *refs)

    return call(finish, (total, y2, scale), (warm.shape, (MODES, MODES)), ((144, 8, 128),))


def solution(mesh):
    finer = Mesh(mesh.devices.reshape(4, 2, 4, 2, 2), (Y, ZL, X, ZH, C))
    placed = (P(GX, YZ, None), P(GX, YZ, None), P(GX, YZ, None), P(None, None, GX, YZ, None))
    return jax.shard_map(
        on_device,
        mesh=finer,
        in_specs=placed,
        out_specs=(P(None, None, GX, YZ, None), P()),
        check_vma=False,
    )
```
